256 devices in a mesh: dp: 32 (over y_lo, z, core), tp: 8 (over y_hi, x).
Axes of the slice: x: 4, y: 4 (y_hi: 2, y_lo: 2; y = y_hi * 2 + y_lo), z: 8, core: 2. Of those that a mesh axis runs over, the one named last changes fastest.
Arguments:
- hidden: bfloat16 [32768, 6144], P('dp', 'tp'), may hold values from -6 to 6
- w_down: bfloat16 [2560, 6144], P('dp', 'tp'), may hold values from -0.078125 to 0.078125
- residual: bfloat16 [32768, 2560], P(('dp', 'tp')), may hold values from -15 to 15
- norm_gain: float32 [2560], replicated, may hold values from 0.5 to 1.5
- norm_bias: float32 [2560], replicated, may hold values from -3 to 3
- keep_flags: int32 [256], replicated, may hold values 0 or 1
- keep_scale: float32 [1], replicated, may hold values from 1.1 to 2
- cotangent: bfloat16 [32768, 2560], P(('dp', 'tp')), may hold values from -24 to 24
Outputs:
- mixed_rows: bfloat16 [32768, 2560], P(('dp', 'tp'))
- normed_rows: bfloat16 [32768, 2560], P('dp')
- grad_hidden: bfloat16 [32768, 6144], P('dp', 'tp')
- grad_down: float32 [2560, 6144], P('dp', 'tp')
The draws below stay inside these ranges and needn't reach their ends.
Inputs may be any that keep to these rules, and one draw needn't show every extreme that they name: `keep_flags`: 1 keeps the image's branch, 0 drops it.
All inputs are finite; a program needn't handle non-finite values.
Results may differ from the reference program's by a relative error of at most 0.014.
Values may be sent and summed in bfloat16 or wider, within the bound.
No kernel may reach another device: no remote copies, remote signals or barrier semaphores. Data moves between devices by JAX's collectives and lax.ppermute only.
A program may use at most 128 MiB of HBM per device.

```python
import jax
import jax.numpy as jnp
from jax import lax

D = 2560
FF = 6144
SEQ = 128
TOKENS = 32768
SAMPLES = 256
N_TP = 8


def draw_residual(key, part):
    key_base, key_rows, key_cols = jax.random.split(key, 3)
    row_scale = jnp.exp(jax.random.uniform(key_rows, (TOKENS, 1), jnp.float32, -0.6, 0.6))
    col_scale = jnp.exp(jax.random.uniform(key_cols, (1, D), jnp.float32, -0.6, 0.6))
    base = jnp.clip(jax.random.normal(key_base, (TOKENS, D), jnp.float32), -4.0, 4.0)
    return (base * row_scale * col_scale).astype(jnp.bfloat16)


def touch_ends(entries, key, low, top_value):
    longest = entries.shape.index(max(entries.shape))
    spots = []
    for shift in (0, 1):
        where = [jax.random.randint(jax.random.fold_in(key, axis), (), 0, length) for axis, length in enumerate(entries.shape)]
        where[longest] = (where[longest] + shift) % entries.shape[longest]
        spots.append(tuple(where))
    return entries.at[spots[0]].set(low).at[spots[1]].set(top_value)


def with_spikes(drawn, stream_key, source, target, blocks, factor):
    owner, partner = [(jnp.arange(drawn.shape[dim]) // (drawn.shape[dim] // blocks)).reshape([-1 if axis == dim else 1 for axis in range(drawn.ndim)]) for dim in (source, target)]
    chosen = jax.random.permutation(stream_key, blocks)[partner]
    strong = (owner == chosen) | (owner == (partner + blocks // 2) % blocks)
    return jnp.where(strong, factor * drawn, drawn)


def block_scale(own_key, extent, shards, smallest, high):
    def one(position, shards_of):
        heights = jax.random.uniform(jax.random.fold_in(jax.random.fold_in(own_key, 6), position), (shards_of,), jnp.float32, smallest / len(shards), high / len(shards))
        return jnp.repeat(jnp.exp(heights), extent[position] // shards_of).reshape((-1,) + (1,) * (len(extent) - position - 1))

    gain = one(*shards[0])
    for cut in shards[1:]:
        gain = gain * one(*cut)
    return gain


def noise(rng, extent, deviation, most, shards=(), kind=jnp.bfloat16):
    values = deviation * jax.random.normal(rng, extent, jnp.float32)
    if shards:
        values = values * block_scale(rng, extent, shards, -0.22, 0.18)
    return jnp.clip(values, -most, most).astype(kind)


def heavy_noise(own_key, extent, width, limit, pieces, heavy, kind=jnp.bfloat16):
    result = width * jax.random.normal(own_key, extent, jnp.float32)
    if pieces:
        result = result * block_scale(own_key, extent, pieces, -0.22, 0.18)
    return jnp.clip(with_spikes(result, jax.random.fold_in(own_key, 3), *heavy), -limit, limit).astype(kind)


def setup_inputs(seed: int = 0) -> dict:
    key_list = jax.random.split(jax.random.key(seed), 9)
    return {
        "hidden": noise(key_list[0], (TOKENS, FF), 1.0, 6.0, ((0, 32), (1, 8))),
        "w_down": noise(key_list[1], (D, FF), FF ** -0.5, 0.078125, ((0, 32), (1, 8))),
        "residual": draw_residual(jax.random.fold_in(key_list[8], 71), 0),
        "norm_gain": jnp.clip(1.0 + 0.1 * jax.random.normal(key_list[3], (D,), jnp.float32), 0.5, 1.5),
        "norm_bias": noise(key_list[4], (D,), 0.5, 3.0, (), jnp.float32),
        "keep_flags": touch_ends((jax.random.randint(key_list[5], (SAMPLES,), 0, 4) < 3).astype(jnp.int32), jax.random.fold_in(key_list[5], 1), 0, 1),
        "keep_scale": jnp.clip(jax.random.uniform(key_list[6], (1,), jnp.float32, 1.1, 2.0), 1.1, 2.0),
        "cotangent": heavy_noise(key_list[7], (TOKENS, D), 1.0, 24.0, ((0, 256),), (0, 1, 256, 6.0)),
    }


def layer_norm(values, norm_gain, norm_bias):
    row_mean = lax.optimization_barrier(jnp.mean(values, axis=-1, keepdims=True))
    centred = values - row_mean
    row_var = lax.optimization_barrier(jnp.mean(centred * centred, axis=-1, keepdims=True))
    return centred * lax.rsqrt(row_var + 1e-06) * norm_gain + norm_bias

def reference(hidden, w_down, residual, norm_gain, norm_bias, keep_flags, keep_scale, cotangent):
    slice_width = FF // N_TP
    sample_ids = jnp.arange(TOKENS, dtype=jnp.int32) // SEQ
    scales = keep_flags[sample_ids].astype(jnp.float32) * keep_scale[0]
    branch = jnp.zeros((TOKENS, D), jnp.float32)
    for member in range(N_TP):
        first_col = member * slice_width
        part_sum = lax.dot_general(hidden[:, first_col:first_col + slice_width], w_down[:, first_col:first_col + slice_width], (((1,), (1,)), ((), ())), preferred_element_type=jnp.float32)
        rounded = lax.optimization_barrier(part_sum.astype(jnp.bfloat16))
        branch = branch + rounded.astype(jnp.float32)
    mixed_rows = (residual.astype(jnp.float32) + scales[:, None] * branch).astype(jnp.bfloat16)
    normed_rows = layer_norm(mixed_rows.astype(jnp.float32), norm_gain, norm_bias).astype(jnp.bfloat16)
    branch_cot = (cotangent.astype(jnp.float32) * scales[:, None]).astype(jnp.bfloat16)
    grad_hidden = jnp.dot(branch_cot, w_down, preferred_element_type=jnp.float32).astype(jnp.bfloat16)
    grad_down = lax.dot_general(branch_cot, hidden, (((0,), (0,)), ((), ())), preferred_element_type=jnp.float32) * (1.0 / SAMPLES)
    return (mixed_rows, normed_rows, grad_hidden, grad_down)
```

```python
import jax
import jax.numpy as jnp
from jax import lax
from jax.sharding import PartitionSpec as P

SEQ = 128
NX, NY = 4, 2
NZ = 8
F32, BF16 = jnp.float32, jnp.bfloat16

X_PERM = {s: [(y * NX + x, y * NX + (x + s) % NX) for y in range(NY) for x in range(NX)] for s in (1, -1)}
Y_PERM = [(y * NX + x, (1 - y) * NX + x) for y in range(NY) for x in range(NX)]


def dp_perm(move):
    return [
        ((l * NZ + z) * 2 + c, move(l, z, c)) for l in range(2) for z in range(NZ) for c in range(2)
    ]


Z_PERM = {s: dp_perm(lambda l, z, c, s=s: (l * NZ + (z + s) % NZ) * 2 + c) for s in (1, -1)}
LO_PERM = dp_perm(lambda l, z, c: ((1 - l) * NZ + z) * 2 + c)
CORE_PERM = dp_perm(lambda l, z, c: (l * NZ + z) * 2 + 1 - c)


def shift_x(v, s):
    return lax.ppermute(v, "tp", X_PERM[s])


def swap_y(v):
    return lax.ppermute(v, "tp", Y_PERM)


def shift_z(v, s):
    return lax.ppermute(v, "dp", Z_PERM[s])


def swap_lo(v):
    return lax.ppermute(v, "dp", LO_PERM)


def swap_core(v):
    return lax.ppermute(v, "dp", CORE_PERM)


def gather_tp(part_a, part_b, place):
    rows_a, rows_b = part_a.shape[0], part_b.shape[0]
    half = rows_b // 16 * 8
    place(0, 0, False, 0, part_a)
    place(0, 0, True, 0, part_b)
    y_a = swap_y(part_a)
    b_left = shift_x(part_b, 1)
    b_right = shift_x(part_b, -1)
    place(1, 0, False, 0, y_a)
    a_two = jnp.concatenate([part_a, y_a])
    a_left = shift_x(a_two, 1)
    a_right = shift_x(a_two, -1)
    place(0, -1, True, 0, b_left)
    place(0, 1, True, 0, b_right)
    b_far_lo = shift_x(b_left[:half], 1)
    b_far_hi = shift_x(b_right[half:], -1)
    y_near = swap_y(jnp.concatenate([part_b, b_left, b_right]))
    place(0, 2, True, 0, b_far_lo)
    place(0, 2, True, half, b_far_hi)
    y_far = swap_y(jnp.concatenate([b_far_lo, b_far_hi]))
    for dy in range(2):
        place(dy, -1, False, 0, a_left[dy * rows_a : (dy + 1) * rows_a])
        place(dy, 1, False, 0, a_right[dy * rows_a : (dy + 1) * rows_a])
    a_far_0 = shift_x(a_left[:rows_a], 1)
    a_far_1 = shift_x(a_right[rows_a:], -1)
    for k, dx in enumerate((0, -1, 1)):
        place(1, dx, True, 0, y_near[k * rows_b : (k + 1) * rows_b])
    place(1, 2, True, 0, y_far)
    place(0, 2, False, 0, a_far_0)
    place(1, 2, False, 0, a_far_1)


class Rows:
    def __init__(self, rows, width, dtype, rows_a):
        self.value = jnp.zeros((NY, NX, rows, width), dtype)
        self.rows_a = rows_a
        me = lax.axis_index("tp").astype(jnp.uint32)
        self.y, self.x = me >> 2, me & 3

    def place(self, dy, dx, is_b, row, piece):
        zero = jnp.uint32(0)
        at = (
            (self.y + dy) & 1,
            (self.x + (dx & 3)) & 3,
            zero + (row + (self.rows_a if is_b else 0)),
            zero,
        )
        self.value = lax.dynamic_update_slice(self.value, piece[None, None], at)


def gather_w(w_down):
    rows, width = w_down.shape
    me = lax.axis_index("dp").astype(jnp.uint32)
    zero = jnp.uint32(0)
    core, z, low = me & 1, (me >> 1) & 7, me >> 4
    whole = jnp.zeros((2, NZ, 2, rows, width), w_down.dtype)
    other = swap_lo(w_down)
    lo_first = low == 0
    pair = jnp.stack([jnp.where(lo_first, w_down, other), jnp.where(lo_first, other, w_down)])

    def put(whole, piece, dz, of_core):
        return lax.dynamic_update_slice(
            whole, piece[:, None, None], (zero, (z + (dz & 7)) & 7, of_core, zero, zero)
        )

    whole = put(whole, pair, 0, core)
    whole = put(whole, swap_core(pair), 0, 1 - core)
    up, down = pair, pair
    for step in range(1, NZ // 2):
        up, down = shift_z(up, 1), shift_z(down, -1)
        whole = put(whole, up, -step, core)
        whole = put(whole, down, step, core)
        both = swap_core(jnp.stack([up, down]))
        whole = put(whole, both[0], -step, 1 - core)
        whole = put(whole, both[1], step, 1 - core)
    far = jnp.concatenate([shift_z(up[:1], 1), shift_z(down[1:], -1)])
    whole = put(whole, far, NZ // 2, core)
    whole = put(whole, swap_core(far), NZ // 2, 1 - core)
    return whole.reshape(-1, width)


def layer_norm(values, norm_gain, norm_bias):
    row_mean = jnp.mean(values, axis=-1, keepdims=True)
    centred = values - row_mean
    row_var = jnp.mean(centred * centred, axis=-1, keepdims=True)
    return centred * lax.rsqrt(row_var + 1e-06) * norm_gain + norm_bias


def add(*parts):
    total = parts[0].astype(F32)
    for part in parts[1:]:
        total = total + part.astype(F32)
    return total


def body(hidden, w_down, residual, norm_gain, norm_bias, keep_flags, keep_scale, cotangent):
    tok, width = residual.shape
    rows_a = tok * 9 // 16
    dp, tp = (lax.axis_index(axis).astype(jnp.uint32) for axis in ("dp", "tp"))
    y, x, zero = tp >> 2, tp & 3, jnp.uint32(0)
    sample = dp * (NX * NY) + tp
    scale = lax.dynamic_slice(keep_flags, (sample,), (1,))[0].astype(F32) * keep_scale[0]

    branch_cot = (cotangent.astype(F32) * scale).astype(BF16)
    cot = Rows(tok, width, BF16, rows_a)
    gather_tp(branch_cot[:rows_a], branch_cot[rows_a:], cot.place)
    cot_all = cot.value.reshape(-1, width)

    whole_down = gather_w(w_down)

    blocks = hidden.reshape(NY, NX, tok, -1)

    def block(dy, dx):
        at = ((y + dy) & 1, (x + (dx & 3)) & 3, zero, zero)
        return lax.dynamic_slice(blocks, at, (1, 1) + blocks.shape[2:])[0, 0]

    rel = {(dy, dx): block(dy, dx) for dy in range(NY) for dx in (-1, 0, 1, 2)}
    order = (2, -1, 1, 0)
    first = jnp.concatenate(
        [rel[0, 2][:rows_a], rel[1, 2][:rows_a]] + [rel[1, dx][rows_a:] for dx in order]
    )
    rest = jnp.concatenate(
        [rel[dy, dx][:rows_a] for dx in (1, -1, 0) for dy in range(NY)]
        + [rel[0, dx][rows_a:] for dx in order]
    )
    contract_last = (((1,), (1,)), ((), ()))

    def partial(rows):
        return lax.dot_general(
            rows, whole_down, contract_last, preferred_element_type=F32
        ).astype(BF16)

    rows_b = tok - rows_a
    half = rows_b // 16 * 8
    p_first = partial(first)
    s0 = shift_x(p_first[:rows_a], 1)
    s1 = shift_x(p_first[rows_a : 2 * rows_a], -1)
    to_y = p_first[2 * rows_a :]
    from_y = jnp.concatenate([swap_y(to_y[: 3 * rows_b]), swap_y(to_y[3 * rows_b :])])
    p_rest = partial(rest)
    p_a = {
        (dy, dx): p_rest[(2 * k + dy) * rows_a : (2 * k + dy + 1) * rows_a]
        for k, dx in enumerate((1, -1, 0))
        for dy in range(NY)
    }
    p_b = p_rest[6 * rows_a :]
    f0 = shift_x(jnp.concatenate([add(p_a[0, 1], s0).astype(BF16), p_a[1, 1]]), 1)
    f1 = shift_x(jnp.concatenate([p_a[0, -1], add(p_a[1, -1], s1).astype(BF16)]), -1)
    q_b = {
        dx: add(p_b[k * rows_b : (k + 1) * rows_b], from_y[k * rows_b : (k + 1) * rows_b])
        for k, dx in enumerate(order)
    }
    t0 = shift_x(q_b[2][:half].astype(BF16), 1)
    t1 = shift_x(q_b[2][half:].astype(BF16), -1)
    other_a = add(p_a[1, 0], f0[rows_a:], f1[rows_a:]).astype(BF16)
    g = swap_y(other_a)
    u0 = shift_x(
        jnp.concatenate([add(q_b[1][:half], t0).astype(BF16), q_b[1][half:].astype(BF16)]), 1
    )
    u1 = shift_x(
        jnp.concatenate([q_b[-1][:half].astype(BF16), add(q_b[-1][half:], t1).astype(BF16)]), -1
    )
    branch_a = add(p_a[0, 0], f0[:rows_a], f1[:rows_a], g)
    branch_b = add(q_b[0], u0, u1)
    mixed_a = (residual[:rows_a].astype(F32) + scale * branch_a).astype(BF16)
    mixed_b = (residual[rows_a:].astype(F32) + scale * branch_b).astype(BF16)
    normed_a = layer_norm(mixed_a.astype(F32), norm_gain, norm_bias).astype(BF16)
    normed_b = layer_norm(mixed_b.astype(F32), norm_gain, norm_bias).astype(BF16)
    normed = Rows(tok, width, BF16, rows_a)
    gather_tp(normed_a, normed_b, normed.place)
    normed_all = normed.value.reshape(-1, width)

    grad_part = lax.dot_general(
        cot_all, hidden, (((0,), (0,)), ((), ())), preferred_element_type=F32
    ).astype(BF16)
    summed = lax.psum_scatter(grad_part, "dp", scatter_dimension=0, tiled=True)
    grad_down = summed.astype(F32) * (1.0 / keep_flags.shape[0])
    grad_hidden = jnp.dot(cot_all, whole_down, preferred_element_type=F32).astype(BF16)
    return (jnp.concatenate([mixed_a, mixed_b]), normed_all, grad_hidden, grad_down)


def solution(mesh):
    in_specs = (
        P("dp", "tp"),
        P("dp", "tp"),
        P(("dp", "tp"), None),
        P(),
        P(),
        P(),
        P(),
        P(("dp", "tp"), None),
    )
    out_specs = (P(("dp", "tp"), None), P("dp", None), P("dp", "tp"), P("dp", "tp"))
    return jax.shard_map(body, mesh=mesh, in_specs=in_specs, out_specs=out_specs, check_vma=False)
```

```python
import jax
import jax.numpy as jnp
from jax import lax
from jax.sharding import Mesh
from jax.sharding import PartitionSpec as P

SEQ = 128
NX, NY = 4, 2
NZ = 8
F32, BF16 = jnp.float32, jnp.bfloat16

AXES = ("lo", "z", "core", "yh", "x")


def shift_x(v, s):
    return lax.ppermute(v, "x", [(i, (i + s) % NX) for i in range(NX)])


def swap(v, axis):
    return lax.ppermute(v, axis, [(0, 1), (1, 0)])


def swap_y(v):
    return swap(v, "yh")


def index(axis):
    return lax.axis_index(axis).astype(jnp.uint32)


def gather_first(part_a, part_b):
    return part_a, part_b, swap_y(part_a), shift_x(part_b, 1), shift_x(part_b, -1)


def gather_rest(first, place):
    part_a, part_b, y_a, b_left, b_right = first
    rows_a, rows_b = part_a.shape[0], part_b.shape[0]
    half = rows_b // 16 * 8
    place(0, 0, False, 0, part_a)
    place(0, 0, True, 0, part_b)
    place(1, 0, False, 0, y_a)
    a_two = jnp.concatenate([part_a, y_a])
    a_left = shift_x(a_two, 1)
    a_right = shift_x(a_two, -1)
    place(0, -1, True, 0, b_left)
    place(0, 1, True, 0, b_right)
    b_far_lo = shift_x(b_left[:half], 1)
    b_far_hi = shift_x(b_right[half:], -1)
    y_near = swap_y(jnp.concatenate([part_b, b_left, b_right]))
    place(0, 2, True, 0, b_far_lo)
    place(0, 2, True, half, b_far_hi)
    y_far = swap_y(jnp.concatenate([b_far_lo, b_far_hi]))
    for dy in range(2):
        place(dy, -1, False, 0, a_left[dy * rows_a : (dy + 1) * rows_a])
        place(dy, 1, False, 0, a_right[dy * rows_a : (dy + 1) * rows_a])
    a_far_0 = shift_x(a_left[:rows_a], 1)
    a_far_1 = shift_x(a_right[rows_a:], -1)
    for k, dx in enumerate((0, -1, 1)):
        place(1, dx, True, 0, y_near[k * rows_b : (k + 1) * rows_b])
    place(1, 2, True, 0, y_far)
    place(0, 2, False, 0, a_far_0)
    place(1, 2, False, 0, a_far_1)


class Rows:
    def __init__(self, value, rows_a):
        self.value = value
        self.rows_a = rows_a
        self.y, self.x = index("yh"), index("x")

    def place(self, dy, dx, is_b, row, piece):
        zero = jnp.uint32(0)
        at = (
            (self.y + dy) & 1,
            (self.x + (dx & 3)) & 3,
            zero + (row + (self.rows_a if is_b else 0)),
            zero,
        )
        self.value = lax.dynamic_update_slice(self.value, piece[None, None], at)


together = lax.optimization_barrier


def low_pair(w_down):
    other = swap(w_down, "lo")
    lo_first = index("lo") == 0
    return jnp.stack([jnp.where(lo_first, w_down, other), jnp.where(lo_first, other, w_down)])


def both_cores(own, far):
    core_first = index("core") == 0
    both = [jnp.where(core_first, own, far), jnp.where(core_first, far, own)]
    return jnp.stack(both, axis=2).transpose(1, 0, 2, 3, 4).reshape(-1, own.shape[-1])


def pick(v, i, axis):
    return lax.dynamic_index_in_dim(v, i, axis, keepdims=False)


def scatter_rest(mine):
    rows, low = mine.shape[2], index("lo")
    mine = mine.reshape(2, NZ * rows, -1)
    mine = lax.psum_scatter(mine, "z", scatter_dimension=1, tiled=True)
    return pick(mine, low, 0) + swap(pick(mine, 1 - low, 0), "lo")


def layer_norm(values, norm_gain, norm_bias):
    row_mean = jnp.mean(values, axis=-1, keepdims=True)
    centred = values - row_mean
    row_var = jnp.mean(centred * centred, axis=-1, keepdims=True)
    return centred * lax.rsqrt(row_var + 1e-06) * norm_gain + norm_bias


def add(*parts):
    total = parts[0].astype(F32)
    for part in parts[1:]:
        total = total + part.astype(F32)
    return total


def body(hidden, w_down, residual, norm_gain, norm_bias, keep_flags, keep_scale, cotangent):
    tok, width = residual.shape
    rows_a = tok * 9 // 16
    y, x, zero = index("yh"), index("x"), jnp.uint32(0)
    sample = index(AXES)
    scale = lax.dynamic_slice(keep_flags, (sample,), (1,))[0].astype(F32) * keep_scale[0]

    pair, cotangent = together((low_pair(w_down), cotangent))
    own_down = lax.all_gather(pair, "z")
    branch_cot = (cotangent.astype(F32) * scale).astype(BF16)
    first = gather_first(branch_cot[:rows_a], branch_cot[rows_a:])
    first, hidden, blank = together((first, hidden, jnp.zeros((), BF16)))
    cot = Rows(jnp.full((NY, NX, tok, width), blank), rows_a)
    gather_rest(first, cot.place)
    cot_all, own_down = together((cot.value, own_down))
    whole_down = both_cores(own_down, swap(own_down, "core"))
    blocks = hidden.reshape(NY, NX, tok, -1)

    def block(dy, dx):
        at = ((y + dy) & 1, (x + (dx & 3)) & 3, zero, zero)
        return lax.dynamic_slice(blocks, at, (1, 1) + blocks.shape[2:])[0, 0]

    rel = {(dy, dx): block(dy, dx) for dy in range(NY) for dx in (-1, 0, 1, 2)}
    order = (-1, 0, 1)
    y_near = jnp.concatenate([rel[1, dx][rows_a:] for dx in order])
    rest = jnp.concatenate(
        [rel[dy, dx][:rows_a] for dx in (1, -1, 0) for dy in range(NY)]
        + [rel[0, dx][rows_a:] for dx in order + (2,)]
    )
    contract_last = (((1,), (1,)), ((), ()))

    def partial(rows):
        return lax.dot_general(
            rows, whole_down, contract_last, preferred_element_type=F32
        ).astype(BF16)

    rows_b = tok - rows_a
    half = rows_b // 16 * 8
    out0, out1, y_far, cot_all, whole_down = together(
        (
            partial(rel[0, 2][:rows_a]),
            partial(rel[1, 2][:rows_a]),
            partial(rel[1, 2][rows_a:]),
            cot_all,
            whole_down,
        )
    )
    s0 = shift_x(out0, 1)
    s1 = shift_x(out1, -1)
    from_y_far = swap_y(y_far)
    p_near = partial(y_near)
    p_rest = partial(rest)
    cot_rows = cot_all.reshape(-1, width)
    grad = lax.dot_general(
        cot_rows, hidden, (((0,), (0,)), ((), ())), preferred_element_type=F32
    )
    cot_all, grad = together((cot_all, grad))
    parts = grad.reshape(2, NZ, 2, w_down.shape[0], -1)
    core = index("core")
    grad_far = swap(pick(parts, 1 - core, 2), "core")
    s0, s1, from_y_far, p_near, p_rest, grad_far = together(
        (s0, s1, from_y_far, p_near, p_rest, grad_far)
    )
    p_a = {
        (dy, dx): p_rest[(2 * k + dy) * rows_a : (2 * k + dy + 1) * rows_a]
        for k, dx in enumerate((1, -1, 0))
        for dy in range(NY)
    }
    p_b = p_rest[6 * rows_a :]
    q_far = add(p_b[3 * rows_b :], from_y_far).astype(BF16)
    out0 = jnp.concatenate([add(p_a[0, 1], s0).astype(BF16), p_a[1, 1], q_far[:half]])
    out1 = jnp.concatenate([p_a[0, -1], add(p_a[1, -1], s1).astype(BF16), q_far[half:]])
    out0, out1, p_near, cot_all, whole_down, grad_far = together(
        (out0, out1, p_near, cot_all, whole_down, grad_far)
    )
    f0 = shift_x(out0, 1)
    f1 = shift_x(out1, -1)
    from_y = swap_y(p_near)
    grad_two = pick(parts, core, 2) + grad_far
    grad_hidden = jnp.dot(
        cot_all.reshape(-1, width), whole_down, preferred_element_type=F32
    ).astype(BF16)
    f0, f1, from_y, grad_hidden, cot_all, grad_two = together(
        (f0, f1, from_y, grad_hidden, cot_all, grad_two)
    )
    summed = scatter_rest(grad_two)
    t0, t1 = f0[2 * rows_a :], f1[2 * rows_a :]
    q_b = {
        dx: add(p_b[k * rows_b : (k + 1) * rows_b], from_y[k * rows_b : (k + 1) * rows_b])
        for k, dx in enumerate(order)
    }
    other_a = add(p_a[1, 0], f0[rows_a : 2 * rows_a], f1[rows_a : 2 * rows_a]).astype(BF16)
    g = swap_y(other_a)
    u0 = shift_x(
        jnp.concatenate([add(q_b[1][:half], t0).astype(BF16), q_b[1][half:].astype(BF16)]), 1
    )
    u1 = shift_x(
        jnp.concatenate([q_b[-1][:half].astype(BF16), add(q_b[-1][half:], t1).astype(BF16)]), -1
    )
    branch_a = add(p_a[0, 0], f0[:rows_a], f1[:rows_a], g)
    branch_b = add(q_b[0], u0, u1)
    mixed_a = (residual[:rows_a].astype(F32) + scale * branch_a).astype(BF16)
    mixed_b = (residual[rows_a:].astype(F32) + scale * branch_b).astype(BF16)
    normed_a = layer_norm(mixed_a.astype(F32), norm_gain, norm_bias).astype(BF16)
    normed_b = layer_norm(mixed_b.astype(F32), norm_gain, norm_bias).astype(BF16)
    normed = Rows(cot_all, rows_a)
    gather_rest(gather_first(normed_a, normed_b), normed.place)
    normed_all = normed.value.reshape(-1, width)

    grad_down = summed * (1.0 / keep_flags.shape[0])
    return (jnp.concatenate([mixed_a, mixed_b]), normed_all, grad_hidden, grad_down)


def solution(mesh):
    inner = Mesh(mesh.devices.reshape(2, NZ, 2, NY, NX), AXES)
    dp, tp = AXES[:3], AXES[3:]
    in_specs = (P(dp, tp), P(dp, tp), P(AXES, None), P(), P(), P(), P(), P(AXES, None))
    out_specs = (P(AXES, None), P(dp, None), P(dp, tp), P(dp, tp))
    return jax.shard_map(body, mesh=inner, in_specs=in_specs, out_specs=out_specs, check_vma=False)
```

```python
import jax
import jax.numpy as jnp
from jax import lax
from jax.sharding import Mesh
from jax.sharding import PartitionSpec as P

SEQ = 128
NX, NY = 4, 2
NZ = 8
F32, BF16 = jnp.float32, jnp.bfloat16

AXES = ("lo", "z", "core", "yh", "x")


def shift_x(v, s):
    return lax.ppermute(v, "x", [(i, (i + s) % NX) for i in range(NX)])


def swap(v, axis):
    return lax.ppermute(v, axis, [(0, 1), (1, 0)])


def swap_y(v):
    return swap(v, "yh")


def index(axis):
    return lax.axis_index(axis).astype(jnp.uint32)


def gather_first(own):
    return own, shift_x(own, 1), shift_x(own, -1), swap_y(own)


def cuts(rows):
    half = rows // 2
    return half, rows * 5 // 16


def send(to_right, to_left, to_side):
    return shift_x(to_right, 1), shift_x(to_left, -1), swap_y(to_side)


def gather_second(first):
    _, left, right, side = first
    h, _ = cuts(left.shape[0])
    return send(
        jnp.concatenate([side[:h], left[:h]]),
        jnp.concatenate([side[:h], right[h:]]),
        jnp.concatenate([left[h:], right[h:]]),
    )


def third_blocks(second):
    up, down, across = second
    h, q = cuts(up.shape[0])
    return up[:q], across[h : h + q], jnp.concatenate([up[h + q :], down[h + q :]])


def place_first(first, place):
    for at, block in zip(((0, 0), (0, -1), (0, 1), (1, 0)), first, strict=True):
        place(*at, block)


def place_second(second, place):
    up, down, across = second
    h, _ = cuts(up.shape[0])
    place(0, 2, jnp.concatenate([up[h:], down[h:]]))
    place(1, -1, jnp.concatenate([up[:h], across[:h]]))
    place(1, 1, jnp.concatenate([down[:h], across[h:]]))


def place_third(third, place):
    far_up, far_down, far_side = third
    part = far_side.shape[0] // 2
    place(1, 2, jnp.concatenate([far_up, far_side[:part], far_down, far_side[part:]]))


class Rows:
    def __init__(self, value):
        self.value = value
        self.y, self.x = index("yh"), index("x")

    def place(self, dy, dx, block):
        zero = jnp.uint32(0)
        at = ((self.y + dy) & 1, (self.x + (dx & 3)) & 3, zero, zero)
        self.value = lax.dynamic_update_slice(self.value, block[None, None], at)


together = lax.optimization_barrier


def low_pair(w_down):
    other = swap(w_down, "lo")
    lo_first = index("lo") == 0
    return jnp.stack([jnp.where(lo_first, w_down, other), jnp.where(lo_first, other, w_down)])


def both_cores(own, far):
    core_first = index("core") == 0
    both = [jnp.where(core_first, own, far), jnp.where(core_first, far, own)]
    return jnp.stack(both, axis=2).transpose(1, 0, 2, 3, 4).reshape(-1, own.shape[-1])


def pick(v, i, axis):
    return lax.dynamic_index_in_dim(v, i, axis, keepdims=False)


def scatter_z(mine):
    rows = mine.shape[2]
    mine = mine.reshape(2, NZ * rows, -1)
    return lax.psum_scatter(mine, "z", scatter_dimension=1, tiled=True)


def scatter_low(mine):
    low = index("lo")
    return pick(mine, low, 0) + swap(pick(mine, 1 - low, 0), "lo")


def layer_norm(values, norm_gain, norm_bias):
    row_mean = jnp.mean(values, axis=-1, keepdims=True)
    centred = values - row_mean
    row_var = jnp.mean(centred * centred, axis=-1, keepdims=True)
    return centred * lax.rsqrt(row_var + 1e-06) * norm_gain + norm_bias


def add(*parts):
    total = parts[0].astype(F32)
    for part in parts[1:]:
        total = total + part.astype(F32)
    return total


def body(hidden, w_down, residual, norm_gain, norm_bias, keep_flags, keep_scale, cotangent):
    tok, width = residual.shape
    y, x, zero = index("yh"), index("x"), jnp.uint32(0)
    sample = index(AXES)
    scale = lax.dynamic_slice(keep_flags, (sample,), (1,))[0].astype(F32) * keep_scale[0]

    pair, cotangent = together((low_pair(w_down), cotangent))
    own_down = lax.all_gather(pair, "z")
    branch_cot = (cotangent.astype(F32) * scale).astype(BF16)
    first = gather_first(branch_cot)
    first, hidden, blank = together((first, hidden, jnp.zeros((), BF16)))
    cot = Rows(jnp.full((NY, NX, tok, width), blank))
    second = gather_second(first)
    place_first(first, cot.place)
    second, own_down = together((second, own_down))
    whole_down = both_cores(own_down, swap(own_down, "core"))

    blocks = hidden.reshape(NY, NX, tok, -1)

    def block(dy, dx):
        at = ((y + dy) & 1, (x + (dx & 3)) & 3, zero, zero)
        return lax.dynamic_slice(blocks, at, (1, 1) + blocks.shape[2:])[0, 0]

    middle = jnp.concatenate([block(1, 1), block(1, -1), block(0, 2)])
    near = jnp.concatenate([block(0, 1), block(0, -1), block(1, 0), block(0, 0)])
    contract_last = (((1,), (1,)), ((), ()))

    def partial(rows):
        return lax.dot_general(
            rows, whole_down, contract_last, preferred_element_type=F32
        ).astype(BF16)

    h, q = cuts(tok)
    far, second, whole_down = together((partial(block(1, 2)), second, whole_down))
    cot_right, cot_left, cot_side = third_blocks(second)
    third = send(
        jnp.concatenate([cot_right, far[:q]]),
        jnp.concatenate([cot_left, far[h : h + q]]),
        jnp.concatenate([cot_side, far[q:h], far[h + q :]]),
    )
    place_second(second, cot.place)
    p_middle, p_near = partial(middle), partial(near)
    third, p_middle, p_near, cot_most = together((third, p_middle, p_near, cot.value))
    cot.value = cot_most
    s_up, s_down, s_side = (v[v.shape[0] // 2 :] for v in third)
    p_right, p_left, p_two = (p_middle[k * tok : (k + 1) * tok] for k in range(3))
    up_in = jnp.concatenate(
        [
            add(p_right[:q], s_up).astype(BF16),
            p_right[q:h],
            p_two[:q],
            add(p_two[q:h], s_side[: h - q]).astype(BF16),
        ]
    )
    down_in = jnp.concatenate(
        [p_left[:h], p_two[h : h + q], add(p_two[h + q :], s_side[h - q :]).astype(BF16)]
    )
    across_in = jnp.concatenate(
        [add(p_left[h : h + q], s_down).astype(BF16), p_left[h + q :], p_right[h:]]
    )
    up_in, down_in, across_in, third, cot.value = together(
        (up_in, down_in, across_in, third, cot.value)
    )
    up, down, across = send(up_in, down_in, across_in)
    place_third([v[: v.shape[0] // 2] for v in third], cot.place)
    cot_all = cot.value
    grad = lax.dot_general(
        cot_all.reshape(-1, width), hidden, (((0,), (0,)), ((), ())), preferred_element_type=F32
    )
    up, down, across, p_near, grad, cot_all = together((up, down, across, p_near, grad, cot_all))
    q_right, q_left, q_side, q_own = (p_near[k * tok : (k + 1) * tok] for k in range(4))
    right_in = jnp.concatenate([add(q_right[:h], up[h:]), add(q_right[h:], across[h:])])
    left_in = jnp.concatenate(
        [q_left[:h], add(q_left[h:], down[h:], across[:h]).astype(BF16)]
    )
    side_in = jnp.concatenate([add(q_side[:h], up[:h], down[:h]).astype(BF16), q_side[h:]])
    right_in, left_in, side_in, grad = together((right_in.astype(BF16), left_in, side_in, grad))
    last = send(right_in, left_in, side_in)
    parts = grad.reshape(2, NZ, 2, w_down.shape[0], -1)
    core = index("core")
    grad_two = add(
        pick(parts, core, 2), swap(pick(parts, 1 - core, 2).astype(BF16), "core")
    )
    grad_chips = scatter_z(grad_two)
    last, cot_all = together((last, cot_all))
    branch = add(q_own, *last)
    mixed = (residual.astype(F32) + scale * branch).astype(BF16)
    normed_own = layer_norm(mixed.astype(F32), norm_gain, norm_bias).astype(BF16)
    normed_own, cot_all, whole_down = together((normed_own, cot_all, whole_down))
    first = gather_first(normed_own)
    grad_hidden = jnp.dot(
        cot_all.reshape(-1, width), whole_down, preferred_element_type=F32
    ).astype(BF16)
    first, grad_hidden, cot_all = together((first, grad_hidden, cot_all))
    normed = Rows(cot_all)
    second = gather_second(first)
    place_first(first, normed.place)
    second, grad_chips = together((second, grad_chips))
    third = send(*third_blocks(second))
    summed = scatter_low(grad_chips)
    place_second(second, normed.place)
    place_third(third, normed.place)
    normed_all = normed.value.reshape(-1, width)

    grad_down = summed * (1.0 / keep_flags.shape[0])
    return (mixed, normed_all, grad_hidden, grad_down)


def solution(mesh):
    inner = Mesh(mesh.devices.reshape(2, NZ, 2, NY, NX), AXES)
    dp, tp = AXES[:3], AXES[3:]
    in_specs = (P(dp, tp), P(dp, tp), P(AXES, None), P(), P(), P(), P(), P(AXES, None))
    out_specs = (P(AXES, None), P(dp, None), P(dp, tp), P(dp, tp))
    return jax.shard_map(body, mesh=inner, in_specs=in_specs, out_specs=out_specs, check_vma=False)
```

```python
import jax
import jax.numpy as jnp
from jax import lax
from jax.sharding import Mesh
from jax.sharding import PartitionSpec as P

SEQ = 128
NX, NY = 4, 2
NZ = 8
F32, BF16 = jnp.float32, jnp.bfloat16

AXES = ("lo", "z", "core", "yh", "x")


def shift_x(v, s):
    return lax.ppermute(v, "x", [(i, (i + s) % NX) for i in range(NX)])


def swap(v, axis):
    return lax.ppermute(v, axis, [(0, 1), (1, 0)])


def swap_y(v):
    return swap(v, "yh")


def index(axis):
    return lax.axis_index(axis).astype(jnp.uint32)


def gather_first(own, early):
    return own, shift_x(own, 1), shift_x(own, -1), swap_y(own[:early])


def send(to_right, to_left, to_side):
    return shift_x(to_right, 1), shift_x(to_left, -1), swap_y(to_side)


def gather_second(first):
    own, left, right, side = first
    h = own.shape[0] // 2
    return send(
        jnp.concatenate([side[:h], left[:h]]),
        jnp.concatenate([side[:h], right[h:]]),
        jnp.concatenate([left[h:], right[h:]]),
    )


def place_first(first, place):
    for at, block in zip(((0, 0), (0, -1), (0, 1)), first, strict=False):
        place(*at, block)


def place_second(second, place):
    up, down, across = second
    h = up.shape[0] // 2
    place(0, 2, jnp.concatenate([up[h:], down[h:]]))
    place(1, -1, jnp.concatenate([up[:h], across[:h]]))
    place(1, 1, jnp.concatenate([down[:h], across[h:]]))


class Rows:
    def __init__(self, value):
        self.value = value
        self.y, self.x = index("yh"), index("x")

    def place(self, dy, dx, block):
        zero = jnp.uint32(0)
        at = ((self.y + dy) & 1, (self.x + (dx & 3)) & 3, zero, zero)
        self.value = lax.dynamic_update_slice(self.value, block[None, None], at)


together = lax.optimization_barrier


def low_pair(w_down):
    other = swap(w_down, "lo")
    lo_first = index("lo") == 0
    return jnp.stack([jnp.where(lo_first, w_down, other), jnp.where(lo_first, other, w_down)])


def both_cores(own, far):
    core_first = index("core") == 0
    both = [jnp.where(core_first, own, far), jnp.where(core_first, far, own)]
    return jnp.stack(both, axis=2).transpose(1, 0, 2, 3, 4).reshape(-1, own.shape[-1])


def pick(v, i, axis):
    return lax.dynamic_index_in_dim(v, i, axis, keepdims=False)


def scatter_z(mine):
    rows = mine.shape[2]
    mine = mine.reshape(2, NZ * rows, -1)
    return lax.psum_scatter(mine, "z", scatter_dimension=1, tiled=True)


def scatter_low(mine):
    low = index("lo")
    return pick(mine, low, 0) + swap(pick(mine, 1 - low, 0), "lo")


def layer_norm(values, norm_gain, norm_bias):
    row_mean = jnp.mean(values, axis=-1, keepdims=True)
    centred = values - row_mean
    row_var = jnp.mean(centred * centred, axis=-1, keepdims=True)
    return centred * lax.rsqrt(row_var + 1e-06) * norm_gain + norm_bias


def add(*parts):
    total = parts[0].astype(F32)
    for part in parts[1:]:
        total = total + part.astype(F32)
    return total


def body(hidden, w_down, residual, norm_gain, norm_bias, keep_flags, keep_scale, cotangent):
    tok, width = residual.shape
    y, x, zero = index("yh"), index("x"), jnp.uint32(0)
    sample = index(AXES)
    scale = lax.dynamic_slice(keep_flags, (sample,), (1,))[0].astype(F32) * keep_scale[0]

    pair, cotangent = together((low_pair(w_down), cotangent))
    own_down = lax.all_gather(pair, "z")
    branch_cot = (cotangent.astype(F32) * scale).astype(BF16)
    first = gather_first(branch_cot, tok)
    first, hidden, blank = together((first, hidden, jnp.zeros((), BF16)))
    cot = Rows(jnp.full((NY, NX, tok, width), blank))
    second = gather_second(first)
    place_first(first, cot.place)
    cot.place(1, 0, first[3])
    second, own_down = together((second, own_down))
    whole_down = both_cores(own_down, swap(own_down, "core"))

    blocks = hidden.reshape(NY, NX, tok, -1)

    def block(dy, dx):
        at = ((y + dy) & 1, (x + (dx & 3)) & 3, zero, zero)
        return lax.dynamic_slice(blocks, at, (1, 1) + blocks.shape[2:])[0, 0]

    middle = jnp.concatenate([block(1, 1), block(1, -1), block(0, 2)])
    h, q, early = tok // 2, tok * 5 // 16, tok * 3 // 4
    side_block = block(1, 0)
    far_rows = jnp.concatenate([block(1, 2), side_block[early:]])
    near = jnp.concatenate([block(0, 1), block(0, -1), block(0, 0), side_block[:early]])
    contract_last = (((1,), (1,)), ((), ()))

    def partial(rows):
        return lax.dot_general(
            rows, whole_down, contract_last, preferred_element_type=F32
        ).astype(BF16)

    far, second, whole_down = together((partial(far_rows), second, whole_down))
    third = send(
        jnp.concatenate([second[0][:h], far[:q]]),
        jnp.concatenate([second[2][h:], far[q : 2 * q]]),
        far[2 * q :],
    )
    place_second(second, cot.place)
    p_middle, p_near = partial(middle), partial(near)
    third, p_middle, p_near, cot_most = together((third, p_middle, p_near, cot.value))
    cot.value = cot_most
    s_up, s_down, s_side = third[0][h:], third[1][h:], third[2][: tok - 2 * q]
    p_right, p_left, p_two = (p_middle[k * tok : (k + 1) * tok] for k in range(3))
    up_in = jnp.concatenate([add(p_right[:q], s_up).astype(BF16), p_right[q:h], p_two[:h]])
    down_in = jnp.concatenate(
        [
            p_left[:q],
            add(p_left[q:h], s_down[: h - q]).astype(BF16),
            p_two[h : 2 * q],
            add(p_two[2 * q :], s_side).astype(BF16),
        ]
    )
    across_in = jnp.concatenate(
        [add(p_left[h : 2 * q], s_down[h - q :]).astype(BF16), p_left[2 * q :], p_right[h:]]
    )
    up_in, down_in, across_in, third, cot.value = together(
        (up_in, down_in, across_in, third, cot.value)
    )
    up, down, across = send(up_in, down_in, across_in)
    cot.place(1, 2, jnp.concatenate([third[0][:h], third[1][:h]]))
    side_late = third[2][tok - 2 * q :]
    cot_all = cot.value
    grad = lax.dot_general(
        cot_all.reshape(-1, width), hidden, (((0,), (0,)), ((), ())), preferred_element_type=F32
    )
    up, down, across, p_near, grad, cot_all = together((up, down, across, p_near, grad, cot_all))
    q_right, q_left, q_own = (p_near[k * tok : (k + 1) * tok] for k in range(3))
    q_side = p_near[3 * tok :]
    right_in = jnp.concatenate([add(q_right[:h], up[h:]), add(q_right[h:], across[h:])])
    left_in = jnp.concatenate(
        [q_left[:h], add(q_left[h:], down[h:], across[:h]).astype(BF16)]
    )
    side_in = jnp.concatenate([add(q_side[:h], up[:h], down[:h]).astype(BF16), q_side[h:]])
    right_in, left_in, side_in, grad = together((right_in.astype(BF16), left_in, side_in, grad))
    last = send(right_in, left_in, side_in)
    parts = grad.reshape(2, NZ, 2, w_down.shape[0], -1)
    core = index("core")
    grad_two = add(
        pick(parts, core, 2), swap(pick(parts, 1 - core, 2).astype(BF16), "core")
    )
    grad_chips = scatter_z(grad_two)
    last, cot_all = together((last, cot_all))
    branch = add(q_own, last[0], last[1], jnp.concatenate([last[2], side_late]))
    mixed = (residual.astype(F32) + scale * branch).astype(BF16)
    normed_own = layer_norm(mixed.astype(F32), norm_gain, norm_bias).astype(BF16)
    normed_own, cot_all, whole_down = together((normed_own, cot_all, whole_down))
    first = gather_first(normed_own, early)
    grad_hidden = jnp.dot(
        cot_all.reshape(-1, width), whole_down, preferred_element_type=F32
    ).astype(BF16)
    first, grad_hidden, cot_all = together((first, grad_hidden, cot_all))
    normed = Rows(cot_all)
    second = gather_second(first)
    place_first(first, normed.place)
    second, grad_chips = together((second, grad_chips))
    up, _, across = second
    third = send(up[:h], across[h:], first[0][early:])
    summed = scatter_low(grad_chips)
    place_second(second, normed.place)
    normed.place(1, 0, jnp.concatenate([first[3], third[2]]))
    normed.place(1, 2, jnp.concatenate([third[0], third[1]]))
    normed_all = normed.value.reshape(-1, width)

    grad_down = summed * (1.0 / keep_flags.shape[0])
    return (mixed, normed_all, grad_hidden, grad_down)


def solution(mesh):
    inner = Mesh(mesh.devices.reshape(2, NZ, 2, NY, NX), AXES)
    dp, tp = AXES[:3], AXES[3:]
    in_specs = (P(dp, tp), P(dp, tp), P(AXES, None), P(), P(), P(), P(), P(AXES, None))
    out_specs = (P(AXES, None), P(dp, None), P(dp, tp), P(dp, tp))
    return jax.shard_map(body, mesh=inner, in_specs=in_specs, out_specs=out_specs, check_vma=False)
```

```python
import jax
import jax.numpy as jnp
from jax import lax
from jax.sharding import Mesh
from jax.sharding import PartitionSpec as P

SEQ = 128
NX, NY = 4, 2
NZ = 8
F32, BF16 = jnp.float32, jnp.bfloat16

AXES = ("lo", "z", "core", "yh", "x")


def shift_x(v, s):
    return lax.ppermute(v, "x", [(i, (i + s) % NX) for i in range(NX)])


def swap(v, axis):
    return lax.ppermute(v, axis, [(0, 1), (1, 0)])


def swap_y(v):
    return swap(v, "yh")


def index(axis):
    return lax.axis_index(axis).astype(jnp.uint32)


def gather_first(own, early):
    return own, shift_x(own, 1), shift_x(own, -1), swap_y(own[:early])


def send(to_right, to_left, to_side):
    return shift_x(to_right, 1), shift_x(to_left, -1), swap_y(to_side)


def gather_second(first):
    own, left, right, side = first
    h = own.shape[0] * 9 // 16
    return send(
        jnp.concatenate([side[:h], left[:h]]),
        jnp.concatenate([side[:h], right[h:]]),
        jnp.concatenate([left[h:], right[h:]]),
    )


def place_first(first, place):
    for at, block in zip(((0, 0), (0, -1), (0, 1)), first, strict=False):
        place(*at, block)


def place_second(second, place):
    up, down, across = second
    h, rest = up.shape[0] // 2, across.shape[0] // 2
    place(0, 2, jnp.concatenate([up[h:], down[h:]]))
    place(1, -1, jnp.concatenate([up[:h], across[:rest]]))
    place(1, 1, jnp.concatenate([down[:h], across[rest:]]))


class Rows:
    def __init__(self, value):
        self.value = value
        self.y, self.x = index("yh"), index("x")

    def place(self, dy, dx, block):
        zero = jnp.uint32(0)
        at = ((self.y + dy) & 1, (self.x + (dx & 3)) & 3, zero, zero)
        self.value = lax.dynamic_update_slice(self.value, block[None, None], at)


together = lax.optimization_barrier


def low_pair(w_down):
    other = swap(w_down, "lo")
    lo_first = index("lo") == 0
    return jnp.stack([jnp.where(lo_first, w_down, other), jnp.where(lo_first, other, w_down)])


def both_cores(own, far):
    core_first = index("core") == 0
    both = [jnp.where(core_first, own, far), jnp.where(core_first, far, own)]
    return jnp.stack(both, axis=2).transpose(1, 0, 2, 3, 4).reshape(-1, own.shape[-1])


def pick(v, i, axis):
    return lax.dynamic_index_in_dim(v, i, axis, keepdims=False)


def scatter_z(mine):
    rows = mine.shape[2]
    mine = mine.reshape(2, NZ * rows, -1)
    return lax.psum_scatter(mine, "z", scatter_dimension=1, tiled=True)


def scatter_low(mine):
    low = index("lo")
    return pick(mine, low, 0) + swap(pick(mine, 1 - low, 0), "lo")


def layer_norm(values, norm_gain, norm_bias):
    row_mean = jnp.mean(values, axis=-1, keepdims=True)
    centred = values - row_mean
    row_var = jnp.mean(centred * centred, axis=-1, keepdims=True)
    return centred * lax.rsqrt(row_var + 1e-06) * norm_gain + norm_bias


def add(*parts):
    total = parts[0].astype(F32)
    for part in parts[1:]:
        total = total + part.astype(F32)
    return total


def body(hidden, w_down, residual, norm_gain, norm_bias, keep_flags, keep_scale, cotangent):
    tok, width = residual.shape
    y, x, zero = index("yh"), index("x"), jnp.uint32(0)
    sample = index(AXES)
    scale = lax.dynamic_slice(keep_flags, (sample,), (1,))[0].astype(F32) * keep_scale[0]

    pair, cotangent = together((low_pair(w_down), cotangent))
    own_down = lax.all_gather(pair, "z")
    branch_cot = (cotangent.astype(F32) * scale).astype(BF16)
    first = gather_first(branch_cot, tok)
    first, hidden, blank = together((first, hidden, jnp.zeros((), BF16)))
    cot = Rows(jnp.full((NY, NX, tok, width), blank))
    second = gather_second(first)
    place_first(first, cot.place)
    cot.place(1, 0, first[3])
    second, own_down = together((second, own_down))
    whole_down = both_cores(own_down, swap(own_down, "core"))

    blocks = hidden.reshape(NY, NX, tok, -1)

    def block(dy, dx):
        at = ((y + dy) & 1, (x + (dx & 3)) & 3, zero, zero)
        return lax.dynamic_slice(blocks, at, (1, 1) + blocks.shape[2:])[0, 0]

    middle = jnp.concatenate([block(1, 1), block(1, -1), block(0, 2)])
    h, q, early = tok * 9 // 16, tok * 5 // 16, tok * 3 // 4
    side_block = block(1, 0)
    far_rows = jnp.concatenate([block(1, 2), side_block[early:]])
    near = jnp.concatenate([block(0, 1), block(0, -1), block(0, 0), side_block[:early]])
    contract_last = (((1,), (1,)), ((), ()))

    def partial(rows):
        return lax.dot_general(
            rows, whole_down, contract_last, preferred_element_type=F32
        ).astype(BF16)

    far, second, whole_down = together((partial(far_rows), second, whole_down))
    third = send(
        jnp.concatenate([second[0][:h], far[:q]]),
        jnp.concatenate([second[2][tok - h :], far[q:h]]),
        far[h:],
    )
    place_second(second, cot.place)
    p_middle, p_near = partial(middle), partial(near)
    third, p_middle, p_near, cot_most = together((third, p_middle, p_near, cot.value))
    cot.value = cot_most
    s_up, s_down, s_side = third[0][h:], third[1][tok - h :], third[2][: tok - h]
    p_right, p_left, p_two = (p_middle[k * tok : (k + 1) * tok] for k in range(3))
    up_in = jnp.concatenate([add(p_right[:q], s_up).astype(BF16), p_right[q:h], p_two[:h]])
    down_in = jnp.concatenate(
        [
            p_left[:q],
            add(p_left[q:h], s_down).astype(BF16),
            add(p_two[h:], s_side).astype(BF16),
        ]
    )
    across_in = jnp.concatenate([p_left[h:], p_right[h:]])
    up_in, down_in, across_in, third, cot.value = together(
        (up_in, down_in, across_in, third, cot.value)
    )
    up, down, across = send(up_in, down_in, across_in)
    cot.place(1, 2, jnp.concatenate([third[0][:h], third[1][: tok - h]]))
    side_late = third[2][tok - h :]
    cot_all = cot.value
    grad = lax.dot_general(
        cot_all.reshape(-1, width), hidden, (((0,), (0,)), ((), ())), preferred_element_type=F32
    )
    up, down, across, p_near, grad, cot_all = together((up, down, across, p_near, grad, cot_all))
    q_right, q_left, q_own = (p_near[k * tok : (k + 1) * tok] for k in range(3))
    q_side = p_near[3 * tok :]
    right_in = jnp.concatenate([add(q_right[:h], up[h:]), add(q_right[h:], across[tok - h :])])
    left_in = jnp.concatenate(
        [q_left[:h], add(q_left[h:], down[h:], across[: tok - h]).astype(BF16)]
    )
    side_in = jnp.concatenate([add(q_side[:h], up[:h], down[:h]).astype(BF16), q_side[h:]])
    right_in, left_in, side_in, grad = together((right_in.astype(BF16), left_in, side_in, grad))
    last = send(right_in, left_in, side_in)
    parts = grad.reshape(2, NZ, 2, w_down.shape[0], -1)
    core = index("core")
    grad_two = add(
        pick(parts, core, 2), swap(pick(parts, 1 - core, 2).astype(BF16), "core")
    )
    grad_chips = scatter_z(grad_two)
    last, cot_all = together((last, cot_all))
    branch = add(q_own, last[0], last[1], jnp.concatenate([last[2], side_late]))
    mixed = (residual.astype(F32) + scale * branch).astype(BF16)
    normed_own = layer_norm(mixed.astype(F32), norm_gain, norm_bias).astype(BF16)
    normed_own, cot_all, whole_down = together((normed_own, cot_all, whole_down))
    first = gather_first(normed_own, early)
    grad_hidden = jnp.dot(
        cot_all.reshape(-1, width), whole_down, preferred_element_type=F32
    ).astype(BF16)
    first, grad_hidden, cot_all = together((first, grad_hidden, cot_all))
    normed = Rows(cot_all)
    second = gather_second(first)
    second, grad_chips, first = together((second, grad_chips, first))
    up, _, across = second
    third = send(up[:h], across[tok - h :], first[0][early:])
    summed = scatter_low(grad_chips)
    place_first(first, normed.place)
    place_second(second, normed.place)
    normed.place(1, 0, jnp.concatenate([first[3], third[2]]))
    normed.place(1, 2, jnp.concatenate([third[0], third[1]]))
    normed_all = normed.value.reshape(-1, width)

    grad_down = summed * (1.0 / keep_flags.shape[0])
    return (mixed, normed_all, grad_hidden, grad_down)


def solution(mesh):
    inner = Mesh(mesh.devices.reshape(2, NZ, 2, NY, NX), AXES)
    dp, tp = AXES[:3], AXES[3:]
    in_specs = (P(dp, tp), P(dp, tp), P(AXES, None), P(), P(), P(), P(), P(AXES, None))
    out_specs = (P(AXES, None), P(dp, None), P(dp, tp), P(dp, tp))
    return jax.shard_map(body, mesh=inner, in_specs=in_specs, out_specs=out_specs, check_vma=False)
```
